256 devices in a mesh: seq: 32 (over x_lo, z, core), wt: 8 (over y, x_hi).
Axes of the slice: x: 4 (x_hi: 2, x_lo: 2; x = x_hi * 2 + x_lo), y: 4, z: 8, core: 2. Of those that a mesh axis runs over, the one named last changes fastest.
Arguments:
- tokens: int32 [8, 4096], P('wt', 'seq'), may hold values from 0 to 511
- embed_table: bfloat16 [512, 8192], P(None, 'wt'), may hold values from -8 to 8
- norm_gain: bfloat16 [8192], P('wt'), may hold values from 0.099609375 to 1.8984375
- w_in: bfloat16 [8192, 3, 4096], P('wt', None, 'seq'), may hold values from -0.0625 to 0.0625
- short_taps: bfloat16 [3, 3, 4096], P(None, None, 'seq'), may hold values from -3 to 3
- filters: bfloat16 [256, 128], P('seq'), may hold values from -2 to 2
- w_out: bfloat16 [8192, 4096], P('wt'), may hold values from -0.09375 to 0.09375
Outputs:
- block_out: bfloat16 [8, 4096, 8192], P(None, 'seq', 'wt')
The draws below stay inside these ranges and needn't reach their ends.
All inputs are finite; a program needn't handle non-finite values.
Results may differ from the reference program's by a relative error of at most 0.0088.
Values may be sent and summed in bfloat16 or wider, within the bound.
A program may use at most 128 MiB of HBM per device.

```python
import math
import jax
import jax.numpy as jnp
import numpy as np
from jax import lax

D = 8192
V = 512
GSZ = 16
FILT = 128
C = 4096
GRP = 256
SEQS = 8
L = 4096


def draw_embed_table(key, part):
    key_base = jax.random.fold_in(key, 21)
    key_cols = jax.random.fold_in(key, 22)
    key_rows = jax.random.fold_in(key, 23)
    feature_pos = jnp.arange(D).astype(jnp.float32) / D
    col_scale = 0.35 * jnp.exp(math.log(3.0) * feature_pos) * jnp.exp(jax.random.uniform(key_cols, (D,), jnp.float32, -0.3, 0.3))
    base_vals = jnp.clip(jax.random.normal(key_base, (V, D), jnp.float32), -3.0, 3.0)
    row_scale = jnp.exp(jax.random.uniform(key_rows, (V, 1), jnp.float32, math.log(0.6), math.log(1.6)))
    return (base_vals * row_scale * col_scale[None, :]).astype(jnp.bfloat16)


def draw_filters(key, part):
    key_rate = jax.random.fold_in(key, 11)
    key_vals = jax.random.fold_in(key, 12)
    log_rate = jax.random.uniform(key_rate, (GRP, 1), jnp.float32, math.log(1.0 / 3000.0), math.log(1.0 / 8.0))
    values = jnp.clip(jax.random.normal(key_vals, (GRP, FILT), jnp.float32), -4.0, 4.0)
    rate = jnp.exp(log_rate)
    positions = jnp.arange(FILT).astype(jnp.float32)[None, :]
    scale = jnp.sqrt(jnp.maximum(2.0 * rate, 1.0 / FILT))
    return (values * jnp.exp(-rate * positions) * scale).astype(jnp.bfloat16)


def plant(array, stream_key, smallest, high):
    shape = array.shape
    place = [jax.random.randint(jax.random.fold_in(stream_key, axis), (), 0, shape[axis]) for axis in range(len(shape))]
    array = array.at[tuple(place)].set(smallest)
    longest = shape.index(max(shape))
    place[longest] = (place[longest] + 1) % shape[longest]
    return array.at[tuple(place)].set(high)


def block_levels(own_key, shape, cuts, least, largest):
    loudness = 1.0
    for position, parts in cuts:
        heights = jax.random.uniform(jax.random.fold_in(jax.random.fold_in(own_key, 6), position), (parts,), jnp.float32, least / len(cuts), largest / len(cuts))
        loudness = loudness * jnp.repeat(jnp.exp(heights), shape[position] // parts).reshape((-1,) + (1,) * (len(shape) - 1 - position))
    return loudness


def rank_table(number_of, slope):
    weights = [(1 << 20) // math.isqrt(standing ** slope) + 1 for standing in range(1, number_of + 1)]
    scale = 1 + sum(weights) // (1 << 30)
    return np.cumsum(np.array([max(1, weight // scale) for weight in weights]))


def ranked(own_key, dims, count, skew):
    grid = rank_table(count, skew)
    ticket = jax.random.randint(jax.random.fold_in(own_key, 1), dims, 0, int(grid[count - 1]))
    grade = jnp.searchsorted(jnp.asarray(grid, jnp.int32), ticket, side="right")
    return jax.random.permutation(jax.random.fold_in(own_key, 2), count)[grade].astype(jnp.int32)


def scatter_about(stream_key, extent, deviation, reach, split=(), held_as=jnp.bfloat16):
    result = jax.random.normal(stream_key, extent, jnp.float32) * deviation
    if len(split) > 0:
        result = block_levels(stream_key, extent, split, -0.22, 0.18) * result
    return jnp.clip(result, min=-reach, max=reach).astype(held_as)


def setup_inputs(seed: int = 0) -> dict:
    splits = jax.random.split(jax.random.key(seed), 8)
    tokens = plant(ranked(splits[0], (SEQS, L), V, 2), jax.random.fold_in(splits[0], 3), 0, V - 1).astype(jnp.int32)
    embed_table = draw_embed_table(jax.random.fold_in(splits[7], 71), 0)
    norm_gain = jnp.clip(1.0 + 0.18 * jax.random.normal(splits[2], (D,), jnp.float32), 0.099609375, 1.8984375).astype(jnp.bfloat16)
    w_in = scatter_about(splits[3], (D, 3, C), D ** -0.5, 0.0625, ((0, 8), (2, 32)))
    short_taps = scatter_about(splits[4], (3, 3, C), 0.6, 3.0, ((2, 32),))
    filters = draw_filters(jax.random.fold_in(splits[7], 71), 0)
    w_out = scatter_about(splits[6], (D, C), C ** -0.5, 0.09375, ((0, 8),))
    return dict(tokens=tokens, embed_table=embed_table, norm_gain=norm_gain, w_in=w_in, short_taps=short_taps, filters=filters, w_out=w_out)


def causal_pair(filter_vals):
    tap_count = filter_vals.shape[1]
    group_count = filter_vals.shape[0]
    tiled_taps = jnp.tile(filter_vals, (1, 2 * tap_count - 1)).reshape(group_count, tap_count, 2 * tap_count - 1)[:, :, :tap_count]
    circulant = jnp.swapaxes(tiled_taps, 1, 2)
    row_pos = lax.broadcasted_iota(jnp.int32, (tap_count, tap_count), 0)
    col_pos = lax.broadcasted_iota(jnp.int32, (tap_count, tap_count), 1)
    lower_mask = (row_pos >= col_pos)[None]
    zero_mat = jnp.zeros_like(circulant)
    return (jnp.where(lower_mask, circulant, zero_mat), jnp.where(lower_mask, zero_mat, circulant))

def reference(tokens, embed_table, norm_gain, w_in, short_taps, filters, w_out):
    table_vals = embed_table.astype(jnp.float32)
    row_scale = lax.rsqrt(lax.optimization_barrier(jnp.mean(table_vals * table_vals, axis=1, keepdims=True)) + 1e-06)
    normed = (table_vals * row_scale * norm_gain.astype(jnp.float32)).astype(jnp.bfloat16)
    vocab_flat = jnp.dot(normed, w_in.reshape(D, 3 * C), preferred_element_type=jnp.float32).astype(jnp.bfloat16)
    vocab_proj = vocab_flat.reshape(V, 3, C)
    tap_vals = short_taps.astype(jnp.float32)
    lower_mat, upper_mat = causal_pair(filters.astype(jnp.float32))

    def one_genome(token_ids):
        embedded = jnp.take(embed_table, token_ids, axis=0)
        projected = jnp.take(vocab_proj, token_ids, axis=0)
        extended = jnp.concatenate([jnp.zeros((2, 3, C), jnp.bfloat16), projected], axis=0).astype(jnp.float32)
        mixture = tap_vals[0] * extended[2:] + tap_vals[1] * extended[1:-1] + tap_vals[2] * extended[:-2]
        product = lax.optimization_barrier((mixture[:, 0] * mixture[:, 2]).astype(jnp.bfloat16)).astype(jnp.float32)
        padded = jnp.concatenate([jnp.zeros((FILT, C), jnp.float32), product], axis=0)
        stacked = padded.reshape(L // FILT + 1, FILT, GRP, GSZ)
        filtered = jnp.einsum('gij,bjgc->bigc', lower_mat, stacked[1:], precision=lax.Precision.HIGHEST)
        filtered = filtered + jnp.einsum('gij,bjgc->bigc', upper_mat, stacked[:-1], precision=lax.Precision.HIGHEST)
        filtered = filtered.reshape(L, C)
        gated = (mixture[:, 1] * filtered).astype(jnp.bfloat16)
        branch = jnp.dot(gated, w_out.T, preferred_element_type=jnp.float32)
        return (embedded.astype(jnp.float32) + branch).astype(jnp.bfloat16)
    return lax.map(one_genome, tokens)
```

```python
import functools

import jax
import jax.numpy as jnp
from jax import lax
from jax.experimental import pallas as pl
from jax.experimental.pallas import tpu as pltpu
from jax.sharding import PartitionSpec as P

F32 = jnp.float32
BF16 = jnp.bfloat16
BLK = 128
GSZ = 16
RING = 4
WT = 2 * RING


def block_kernel(
    nseq,
    feature_count,
    tok_ref,
    emb_ref,
    gain_ref,
    win_ref,
    taps_ref,
    base_ref,
    wout_hbm,
    out_ref,
    wout,
    part_out,
    part_in,
    sq_out,
    sq_in,
    vtab,
    tok_seq,
    tok_wt,
    toep,
    ext,
    carry,
    sbuf,
    gath,
    acc,
    wout_sem,
    self_sem,
    p_send,
    p_recv,
    q_send,
    q_recv,
    v_send,
    v_recv,
    ts_send,
    ts_recv,
    tw_send,
    tw_recv,
    s1,
    r1,
    sx,
    rx,
    sy,
    ry,
):
    nchip = nseq // 2
    seq = lax.axis_index("seq")
    wt = lax.axis_index("wt")
    chip, core = seq // 2, seq % 2
    y, xh = wt // 2, wt % 2
    vocab = emb_ref.shape[0]
    vrow = vocab // WT
    wide = 3 * BLK

    def genome(dy, flip):
        return ((y + dy + RING) % RING) * 2 + (xh if flip == 0 else 1 - xh)

    def remote(src, dst, ssem, rsem, where):
        return pltpu.make_async_remote_copy(
            src_ref=src,
            dst_ref=dst,
            send_sem=ssem,
            recv_sem=rsem,
            device_id=where,
            device_id_type=pl.DeviceIdType.MESH,
        )

    def seq_peer(d):
        return {"seq": (seq + d) % nseq}

    def wt_peer(d):
        return {"wt": (wt + d) % WT}

    barrier = pltpu.get_barrier_semaphore()

    @pl.loop(1, nseq)
    def _(d):
        pl.semaphore_signal(
            barrier, inc=1, device_id=seq_peer(d), device_id_type=pl.DeviceIdType.MESH
        )

    @pl.loop(1, WT)
    def _(d):
        pl.semaphore_signal(
            barrier, inc=1, device_id=wt_peer(d), device_id_type=pl.DeviceIdType.MESH
        )

    load_wout = pltpu.make_async_copy(wout_hbm, wout, wout_sem)
    load_wout.start()

    sq_out[...] = jnp.zeros_like(sq_out)
    rows = vocab // 2

    @pl.loop(0, 2)
    def _(i):
        e = emb_ref[pl.ds(pl.multiple_of(i * rows, rows), rows), :].astype(F32)
        sq = jnp.sum(e * e, axis=1, keepdims=True)
        r = lax.broadcasted_iota(jnp.int32, (rows, vocab), 0) + i * rows
        l = lax.broadcasted_iota(jnp.int32, (rows, vocab), 1)
        sq_out[...] += jnp.sum(jnp.where(r == l, sq, 0.0), axis=0, keepdims=True)
        gained = (e * gain_ref[...].astype(F32)).astype(BF16)
        p = jnp.dot(gained, win_ref[...], preferred_element_type=F32).astype(BF16)
        for k in range(WT // 2):
            part_out[i * (WT // 2) + k] = p[k * vrow : (k + 1) * vrow]

    tok_seq[seq] = tok_ref[...]
    tok_wt[wt] = tok_ref[...]

    pl.semaphore_wait(barrier, nseq - 1 + WT - 1)

    def part_copy(d):
        return remote(
            part_out.at[(wt + d) % WT], part_in.at[d], p_send.at[d], p_recv.at[d], wt_peer(d)
        )

    def sq_copy(d):
        return remote(sq_out, sq_in.at[d], q_send.at[d], q_recv.at[d], wt_peer(d))

    def tok_wt_copy(d):
        return remote(tok_ref, tok_wt.at[wt], tw_send.at[d], tw_recv.at[d], wt_peer(d))

    def tok_seq_copy(d):
        return remote(tok_ref, tok_seq.at[seq], ts_send.at[d], ts_recv.at[d], seq_peer(d))

    @pl.loop(1, WT)
    def _(d):
        sq_copy(d).start()
        part_copy(d).start()

    @pl.loop(1, WT)
    def _(d):
        tok_wt_copy(d).start()

    @pl.loop(1, nseq)
    def _(d):
        tok_seq_copy(d).start()

    @pl.loop(0, BLK // GSZ)
    def _(q):
        row = jnp.broadcast_to(base_ref[pl.ds(q, 1), :], (BLK, 2 * BLK))
        toep[pl.ds(pl.multiple_of(q * BLK, BLK), BLK), :] = pltpu.roll(
            row, 0, 1, stride=1, stride_axis=0
        ).astype(BF16)

    @pl.loop(1, WT)
    def _(d):
        sq_copy(d).wait_recv()
        part_copy(d).wait_recv()

    total = part_out[wt].astype(F32)
    squares = sq_out[...]
    for d in range(1, WT):
        total = total + part_in[d].astype(F32)
        squares = squares + sq_in[d]
    scale = lax.rsqrt(squares / feature_count + 1e-06)
    r = lax.broadcasted_iota(jnp.int32, (vrow, vocab), 0) + wt * vrow
    l = lax.broadcasted_iota(jnp.int32, (vrow, vocab), 1)
    scale_col = jnp.sum(jnp.where(r == l, scale, 0.0), axis=1, keepdims=True)
    vtab[wt] = (total * scale_col).astype(BF16)

    def vocab_copy(d):
        return remote(vtab.at[wt], vtab.at[wt], v_send.at[d], v_recv.at[d], wt_peer(d))

    def vocab_arrival(d):
        whence = (wt - d + WT) % WT
        return remote(
            vtab.at[whence], vtab.at[whence], v_send.at[d], v_recv.at[d], wt_peer(d)
        )

    @pl.loop(1, WT)
    def _(d):
        vocab_copy(d).start()

    def one_hot(row):
        cols = jnp.broadcast_to(row, (BLK, BLK)).T
        lane = lax.broadcasted_iota(jnp.int32, (BLK, BLK), 1)
        return jnp.concatenate(
            [
                jnp.where(cols == lane + k * BLK, 1.0, 0.0).astype(BF16)
                for k in range(vocab // BLK)
            ],
            axis=1,
        )

    @pl.loop(1, WT)
    def _(d):
        whence = (wt - d + WT) % WT
        remote(
            tok_ref, tok_wt.at[whence], tw_send.at[d], tw_recv.at[d], wt_peer(d)
        ).wait_recv()

    @pl.loop(0, WT // 2)
    def _(g):
        hot = jnp.concatenate([one_hot(tok_wt[2 * g]), one_hot(tok_wt[2 * g + 1])], axis=0)
        acc[pl.ds(pl.multiple_of(g * 2 * BLK, 2 * BLK), 2 * BLK), :] = jnp.dot(
            hot, emb_ref[...], preferred_element_type=F32
        )

    @pl.loop(1, nseq)
    def _(d):
        whence = (seq - d + nseq) % nseq
        remote(
            tok_ref, tok_seq.at[whence], ts_send.at[d], ts_recv.at[d], seq_peer(d)
        ).wait_recv()

    load_wout.wait()

    @pl.loop(1, WT)
    def _(d):
        vocab_arrival(d).wait_recv()

    ext[...] = jnp.zeros_like(ext)
    carry[...] = jnp.zeros_like(carry)

    def block_send(u, i):
        to = 2 * ((chip + u) % nchip) + i
        return remote(
            sbuf.at[u, i],
            gath.at[u, wt, :, pl.ds(pl.multiple_of(core * BLK, BLK), BLK)],
            s1.at[u, i],
            r1.at[u, core],
            {"seq": to},
        )

    def block_local(i):
        return pltpu.make_async_copy(
            sbuf.at[0, i],
            gath.at[0, wt, :, pl.ds(pl.multiple_of(core * BLK, BLK), BLK)],
            self_sem,
        )

    def block_arrival(u, i):
        return remote(
            sbuf.at[u, i],
            gath.at[u, wt, :, pl.ds(i * BLK, BLK)],
            s1.at[u, i],
            r1.at[u, i],
            {"seq": 2 * ((chip + u) % nchip) + i},
        )

    def mixer(u):
        at = (chip + u + nchip) % nchip

        @pl.when(at == 0)
        def _():
            ext[0:8, :] = jnp.zeros((8, wide), F32)
            carry[...] = jnp.zeros_like(carry)

        hot = jnp.concatenate([one_hot(tok_seq[2 * at]), one_hot(tok_seq[2 * at + 1])], axis=0)
        ext[8 : 8 + 2 * BLK, :] = jnp.dot(
            hot, vtab[...].reshape(vocab, wide), preferred_element_type=F32
        )

        def mixed(s):
            lanes = slice(s * BLK, (s + 1) * BLK)
            return (
                taps_ref[0:1, lanes] * ext[8 : 8 + 2 * BLK, lanes]
                + taps_ref[1:2, lanes] * ext[7 : 7 + 2 * BLK, lanes]
                + taps_ref[2:3, lanes] * ext[6 : 6 + 2 * BLK, lanes]
            )

        inner = (mixed(0) * mixed(2)).astype(BF16)
        middle = mixed(1)
        first, second = inner[:BLK], inner[BLK:]
        pair = jnp.concatenate(
            [
                jnp.concatenate([carry[...], first], axis=1),
                jnp.concatenate([first, second], axis=1),
            ],
            axis=0,
        )
        filtered = jnp.dot(toep[...], pair, preferred_element_type=F32)
        group = (lax.broadcasted_iota(jnp.int32, (BLK, 2 * BLK), 1) % BLK) // GSZ
        conv = filtered[0:BLK]
        for q in range(1, BLK // GSZ):
            conv = jnp.where(group == q, filtered[q * BLK : (q + 1) * BLK], conv)
        carry[...] = second
        ext[0:8, :] = ext[2 * BLK : 2 * BLK + 8, :]

        @pl.when(u >= 0)
        def _():
            sbuf[u, 0] = (middle[:BLK] * conv[:, :BLK]).astype(BF16)
            sbuf[u, 1] = (middle[BLK:] * conv[:, BLK:]).astype(BF16)
            for i in range(2):
                mine = (u == 0) & (core == i)

                @pl.when(mine)
                def _():
                    block_local(i).start()

                @pl.when(jnp.logical_not(mine))
                def _():
                    block_send(u, i).start()

    def x_copy(u, g):
        return remote(
            gath.at[u, g], gath.at[u, g], sx.at[u], rx.at[u], {"wt": genome(0, 1)}
        )

    def y_copy(u, way, kind, g):
        k = (u * 2 + way) * 3 + kind
        to = genome(1 if way == 0 else -1, 0)
        return remote(gath.at[u, g], gath.at[u, g], sy.at[k], ry.at[k], {"wt": to})

    def spread(u):
        for i in range(2):
            mine = (u == 0) & (core == i)

            @pl.when(mine)
            def _():
                block_local(i).wait()

            @pl.when(jnp.logical_not(mine))
            def _():
                block_arrival(u, i).wait_recv()

        y_copy(u, 0, 0, wt).start()
        y_copy(u, 1, 0, wt).start()
        x_copy(u, wt).start()

    def spread_partner(u):
        other = genome(0, 1)
        x_copy(u, other).wait_recv()
        y_copy(u, 0, 1, other).start()
        y_copy(u, 1, 1, other).start()

    def relay(u):
        behind = genome(-1, 0)
        y_copy(u, 0, 0, behind).wait_recv()
        y_copy(u, 0, 2, behind).start()
        ahead = genome(1, 1)
        y_copy(u, 1, 1, ahead).wait_recv()
        y_copy(u, 1, 2, ahead).start()

    def project(u):
        y_copy(u, 0, 1, genome(-1, 1)).wait_recv()
        y_copy(u, 1, 0, genome(1, 0)).wait_recv()
        y_copy(u, 0, 2, genome(-2, 0)).wait_recv()
        y_copy(u, 1, 2, genome(2, 1)).wait_recv()
        owner = (chip - u + nchip) % nchip
        cols = pl.ds(pl.multiple_of(owner * 2 * BLK, 2 * BLK), 2 * BLK)
        held = gath[u].reshape(WT * BLK, 2 * BLK)
        tile = min(256, acc.shape[1])

        @pl.loop(0, acc.shape[1] // tile)
        def _(n):
            at = pl.ds(pl.multiple_of(n * tile, tile), tile)
            acc[:, at] += lax.dot_general(
                held, wout[at, cols], (((1,), (1,)), ((), ())), preferred_element_type=F32
            )

    @pl.loop(-1, nchip + 4)
    def _(t):
        @pl.when(t < nchip)
        def _():
            mixer(t)

        for lag, stage in ((1, spread), (2, spread_partner), (3, relay), (4, project)):

            @pl.when((t >= lag) & (t < nchip + lag))
            def _():
                stage(t - lag)

    @pl.loop(0, WT)
    def _(g):
        out_ref[g] = acc[pl.ds(pl.multiple_of(g * BLK, BLK), BLK), :].astype(BF16)

    @pl.loop(1, WT)
    def _(d):
        sq_copy(d).wait_send()
        part_copy(d).wait_send()
        tok_wt_copy(d).wait_send()
        vocab_copy(d).wait_send()

    @pl.loop(1, nseq)
    def _(d):
        tok_seq_copy(d).wait_send()

    @pl.loop(0, nchip)
    def _(u):
        for i in range(2):

            @pl.when(jnp.logical_not((u == 0) & (core == i)))
            def _():
                block_send(u, i).wait_send()

        x_copy(u, wt).wait_send()
        for kind in range(3):
            for way in range(2):
                y_copy(u, way, kind, wt).wait_send()


def local(nseq, tokens, embed_table, norm_gain, w_in, short_taps, filters, w_out):
    vocab, feats = embed_table.shape
    taps = filters.shape[1]
    base = jnp.pad(filters[:, ::-1].astype(F32), ((0, 0), (1, taps - 1)))
    nchip = nseq // 2
    wide = 3 * BLK
    dma = pltpu.SemaphoreType.DMA
    vmem = pl.BlockSpec(memory_space=pltpu.VMEM)
    return pl.pallas_call(
        functools.partial(block_kernel, nseq, feats * WT),
        out_shape=jax.ShapeDtypeStruct((WT, BLK, feats), BF16),
        in_specs=[vmem] * 6 + [pl.BlockSpec(memory_space=pl.ANY)],
        out_specs=vmem,
        scratch_shapes=[
            pltpu.VMEM(w_out.shape, BF16),
            pltpu.VMEM((WT, vocab // WT, wide), BF16),
            pltpu.VMEM((WT, vocab // WT, wide), BF16),
            pltpu.VMEM((1, vocab), F32),
            pltpu.VMEM((WT, 1, vocab), F32),
            pltpu.VMEM((WT, vocab // WT, wide), BF16),
            pltpu.VMEM((nseq, 1, BLK), jnp.int32),
            pltpu.VMEM((WT, 1, BLK), jnp.int32),
            pltpu.VMEM((BLK // GSZ * BLK, 2 * BLK), BF16),
            pltpu.VMEM((8 + 2 * BLK, wide), F32),
            pltpu.VMEM((BLK, BLK), BF16),
            pltpu.VMEM((nchip, 2, BLK, BLK), BF16),
            pltpu.VMEM((nchip, WT, BLK, 2 * BLK), BF16),
            pltpu.VMEM((WT * BLK, feats), F32),
            dma,
            dma,
            dma((WT,)),
            dma((WT,)),
            dma((WT,)),
            dma((WT,)),
            dma((WT,)),
            dma((WT,)),
            dma((nseq,)),
            dma((nseq,)),
            dma((WT,)),
            dma((WT,)),
            dma((nchip, 2)),
            dma((nchip, 2)),
            dma((nchip,)),
            dma((nchip,)),
            dma((nchip * 6,)),
            dma((nchip * 6,)),
        ],
        compiler_params=pltpu.CompilerParams(collective_id=0, has_side_effects=True),
        name="hyena_block",
    )(
        tokens,
        embed_table,
        norm_gain.reshape(1, feats),
        w_in.reshape(feats, wide),
        short_taps.astype(F32).reshape(3, wide),
        base,
        w_out,
    )


def solution(mesh):
    placed = (
        P("wt", "seq"),
        P(None, "wt"),
        P("wt"),
        P("wt", None, "seq"),
        P(None, None, "seq"),
        P("seq", None),
        P("wt", None),
    )
    return jax.shard_map(
        functools.partial(local, mesh.shape["seq"]),
        mesh=mesh,
        in_specs=placed,
        out_specs=P(None, "seq", "wt"),
        check_vma=False,
    )
```

```python
import functools

import jax
import jax.numpy as jnp
from jax import lax
from jax.experimental import pallas as pl
from jax.experimental.pallas import tpu as pltpu
from jax.sharding import PartitionSpec as P

F32 = jnp.float32
BF16 = jnp.bfloat16
BLK = 128
GSZ = 16
HALO = 16
RING = 4
WT = 2 * RING


def block_kernel(
    nseq,
    feature_count,
    tok_ref,
    emb_ref,
    gain_ref,
    win_ref,
    taps_ref,
    filt_ref,
    wout_hbm,
    out_ref,
    wout,
    part_out,
    part_in,
    sq_out,
    sq_in,
    vtab,
    tok_seq,
    tok_wt,
    toep,
    ext,
    sbuf,
    gath,
    acc,
    wout_sem,
    self_sem,
    p_send,
    p_recv,
    q_send,
    q_recv,
    v_send,
    v_recv,
    ts_send,
    ts_recv,
    tw_send,
    tw_recv,
    s1,
    r1,
    sx,
    rx,
    sy,
    ry,
):
    nchip, nz = nseq // 2, nseq // 4
    seq = lax.axis_index("seq")
    wt = lax.axis_index("wt")
    chip, core = seq // 2, seq % 2
    y, xh = wt // 2, wt % 2
    vocab = emb_ref.shape[0]
    vrow = vocab // WT
    wide = 3 * BLK

    def genome(dy, flip):
        return ((y + dy + RING) % RING) * 2 + (xh if flip == 0 else 1 - xh)

    def remote(src, dst, ssem, rsem, where):
        return pltpu.make_async_remote_copy(
            src_ref=src,
            dst_ref=dst,
            send_sem=ssem,
            recv_sem=rsem,
            device_id=where,
            device_id_type=pl.DeviceIdType.MESH,
        )

    def seq_peer(d):
        return {"seq": (seq + d) % nseq}

    def wt_peer(d):
        return {"wt": (wt + d) % WT}

    barrier = pltpu.get_barrier_semaphore()

    @pl.loop(1, nseq)
    def _(d):
        pl.semaphore_signal(
            barrier, inc=1, device_id=seq_peer(d), device_id_type=pl.DeviceIdType.MESH
        )

    @pl.loop(1, WT)
    def _(d):
        pl.semaphore_signal(
            barrier, inc=1, device_id=wt_peer(d), device_id_type=pl.DeviceIdType.MESH
        )

    load_wout = pltpu.make_async_copy(wout_hbm, wout, wout_sem)
    load_wout.start()

    sq_out[...] = jnp.zeros_like(sq_out)
    rows = vocab // 2

    @pl.loop(0, 2)
    def _(i):
        e = emb_ref[pl.ds(pl.multiple_of(i * rows, rows), rows), :].astype(F32)
        sq = jnp.sum(e * e, axis=1, keepdims=True)
        r = lax.broadcasted_iota(jnp.int32, (rows, vocab), 0) + i * rows
        l = lax.broadcasted_iota(jnp.int32, (rows, vocab), 1)
        sq_out[...] += jnp.sum(jnp.where(r == l, sq, 0.0), axis=0, keepdims=True)
        gained = (e * gain_ref[...].astype(F32).reshape(1, -1)).astype(BF16)
        streams = jnp.concatenate([win_ref[k] for k in range(3)], axis=1)
        p = jnp.dot(gained, streams, preferred_element_type=F32).astype(BF16)
        for k in range(WT // 2):
            part_out[i * (WT // 2) + k] = p[k * vrow : (k + 1) * vrow]

    filt = filt_ref[...].astype(F32)
    for q in range(BLK // GSZ):
        row = jnp.concatenate([filt[q : q + 1], jnp.zeros((1, BLK), F32)], axis=1)
        rolled = pltpu.roll(
            jnp.broadcast_to(row, (2 * BLK, 2 * BLK)), BLK, 1, stride=1, stride_axis=0
        )
        toep[q * BLK : (q + 1) * BLK, :] = rolled[:, :BLK].T.astype(BF16)

    tok_seq[seq] = tok_ref[...]
    tok_wt[wt] = tok_ref[...]

    pl.semaphore_wait(barrier, nseq - 1 + WT - 1)

    def part_copy(d):
        return remote(
            part_out.at[(wt + d) % WT], part_in.at[d], p_send.at[d], p_recv.at[d], wt_peer(d)
        )

    def sq_copy(d):
        return remote(sq_out, sq_in.at[d], q_send.at[d], q_recv.at[d], wt_peer(d))

    def tok_wt_copy(d):
        return remote(tok_ref, tok_wt.at[wt], tw_send.at[d], tw_recv.at[d], wt_peer(d))

    def tok_seq_copy(d):
        return remote(tok_ref, tok_seq.at[seq], ts_send.at[d], ts_recv.at[d], seq_peer(d))

    @pl.loop(1, WT)
    def _(d):
        sq_copy(d).start()
        part_copy(d).start()

    @pl.loop(1, WT)
    def _(d):
        tok_wt_copy(d).start()

    @pl.loop(1, nseq)
    def _(d):
        tok_seq_copy(d).start()

    @pl.loop(1, WT)
    def _(d):
        sq_copy(d).wait_recv()
        part_copy(d).wait_recv()

    total = part_out[wt].astype(F32)
    squares = sq_out[...]
    for d in range(1, WT):
        total = total + part_in[d].astype(F32)
        squares = squares + sq_in[d]
    scale = lax.rsqrt(squares / feature_count + 1e-06)
    r = lax.broadcasted_iota(jnp.int32, (vrow, vocab), 0) + wt * vrow
    l = lax.broadcasted_iota(jnp.int32, (vrow, vocab), 1)
    scale_col = jnp.sum(jnp.where(r == l, scale, 0.0), axis=1, keepdims=True)
    vtab[wt] = (total * scale_col).astype(BF16)

    def vocab_copy(d):
        return remote(vtab.at[wt], vtab.at[wt], v_send.at[d], v_recv.at[d], wt_peer(d))

    def vocab_arrival(d):
        whence = (wt - d + WT) % WT
        return remote(
            vtab.at[whence], vtab.at[whence], v_send.at[d], v_recv.at[d], wt_peer(d)
        )

    @pl.loop(1, WT)
    def _(d):
        vocab_copy(d).start()

    def one_hot(row):
        cols = jnp.broadcast_to(row, (BLK, BLK)).T
        lane = lax.broadcasted_iota(jnp.int32, (BLK, BLK), 1)
        return jnp.concatenate(
            [
                jnp.where(cols == lane + k * BLK, 1.0, 0.0).astype(BF16)
                for k in range(vocab // BLK)
            ],
            axis=1,
        )

    @pl.loop(1, nseq)
    def _(d):
        whence = (seq - d + nseq) % nseq
        remote(
            tok_ref, tok_seq.at[whence], ts_send.at[d], ts_recv.at[d], seq_peer(d)
        ).wait_recv()

    @pl.loop(1, WT)
    def _(d):
        vocab_arrival(d).wait_recv()

    steps = [0, 2, -2, 3, -3, 4, 1, -1] if nz == 8 else list(range(nz))

    def offset(u):
        step = sum(jnp.where(u // 2 == k, v, 0) for k, v in enumerate(steps) if v != 0)
        return u % 2, step

    def chip_at(u, sign):
        flip, step = offset(u)
        xl, z = chip // nz, chip % nz
        return ((xl + flip) % 2) * nz + (z + sign * step + nz) % nz

    def block_send(u, i):
        to = 2 * chip_at(u, 1) + i
        return remote(
            sbuf.at[u, i],
            gath.at[u, wt, :, pl.ds(pl.multiple_of(core * BLK, BLK), BLK)],
            s1.at[u, i],
            r1.at[u, core],
            {"seq": to},
        )

    def block_local(i):
        return pltpu.make_async_copy(
            sbuf.at[0, i],
            gath.at[0, wt, :, pl.ds(pl.multiple_of(core * BLK, BLK), BLK)],
            self_sem,
        )

    def block_arrival(u, i):
        return remote(
            sbuf.at[u, i],
            gath.at[u, wt, :, pl.ds(i * BLK, BLK)],
            s1.at[u, i],
            r1.at[u, i],
            {"seq": 2 * chip_at(u, 1) + i},
        )

    def mixer(u):
        at = chip_at(u, 1)
        before = (2 * at - 2 + nseq) % nseq
        hot = jnp.concatenate(
            [one_hot(tok_seq[before])[BLK - HALO :]]
            + [one_hot(tok_seq[(before + k) % nseq]) for k in range(1, 4)],
            axis=0,
        )
        proj = jnp.dot(hot, vtab[...].reshape(vocab, wide), preferred_element_type=F32)
        past = HALO + BLK
        ext[:past, :] = jnp.where(at > 0, proj[:past], 0.0)
        ext[past:, :] = proj[past:]

        def mixed(s, start, rows):
            lanes = slice(s * BLK, (s + 1) * BLK)
            return sum(
                taps_ref[k][s : s + 1].astype(F32) * ext[start - k : start - k + rows, lanes]
                for k in range(3)
            )

        inner = (mixed(0, HALO, 3 * BLK) * mixed(2, HALO, 3 * BLK)).astype(BF16)
        middle = mixed(1, past, 2 * BLK)
        prior, first, second = (inner[k * BLK : (k + 1) * BLK] for k in range(3))
        pair = jnp.concatenate(
            [
                jnp.concatenate([prior, first], axis=1),
                jnp.concatenate([first, second], axis=1),
            ],
            axis=0,
        )
        filtered = jnp.dot(toep[...], pair, preferred_element_type=F32)
        group = (lax.broadcasted_iota(jnp.int32, (BLK, 2 * BLK), 1) % BLK) // GSZ
        conv = filtered[0:BLK]
        for q in range(1, BLK // GSZ):
            conv = jnp.where(group == q, filtered[q * BLK : (q + 1) * BLK], conv)
        sbuf[u, 0] = (middle[:BLK] * conv[:, :BLK]).astype(BF16)
        sbuf[u, 1] = (middle[BLK:] * conv[:, BLK:]).astype(BF16)
        for i in range(2):
            mine = (u == 0) & (core == i)

            @pl.when(mine)
            def _():
                block_local(i).start()

            @pl.when(jnp.logical_not(mine))
            def _():
                block_send(u, i).start()

    def x_copy(u, kind, g):
        k = u * 4 + kind
        return remote(
            gath.at[u, g], gath.at[u, g], sx.at[k], rx.at[k], {"wt": genome(0, 1)}
        )

    def y_copy(u, way, kind, g, half=False):
        k = (u * 2 + way) * 3 + kind
        to = genome(1 if way == 0 else -1, 0)
        part = gath.at[u, g]
        if half:
            part = gath.at[u, g, way * (BLK // 2) : (way + 1) * (BLK // 2)]
        return remote(part, part, sy.at[k], ry.at[k], {"wt": to})

    def late(u):
        return u % 3 == 1

    def spread(u):
        for i in range(2):
            mine = (u == 0) & (core == i)

            @pl.when(mine)
            def _():
                block_local(i).wait()

            @pl.when(jnp.logical_not(mine))
            def _():
                block_arrival(u, i).wait_recv()

        y_copy(u, 0, 0, wt).start()
        y_copy(u, 1, 0, wt).start()
        x_copy(u, 0, wt).start()

    def relay(u):
        @pl.when(jnp.logical_not(late(u)))
        def _():
            other = genome(0, 1)
            x_copy(u, 0, other).wait_recv()
            y_copy(u, 0, 1, other).start()
            y_copy(u, 1, 1, other).start()

        @pl.when(late(u))
        def _():
            for way, dy in ((0, -1), (1, 1)):
                g = genome(dy, 0)
                y_copy(u, way, 0, g).wait_recv()
                y_copy(u, way, 2, g, half=True).start()
                x_copy(u, 1 + way, g).start()

    def relay_again(u):
        @pl.when(jnp.logical_not(late(u)))
        def _():
            behind = genome(-1, 0)
            y_copy(u, 0, 0, behind).wait_recv()
            y_copy(u, 0, 2, behind).start()
            ahead = genome(1, 1)
            y_copy(u, 1, 1, ahead).wait_recv()
            y_copy(u, 1, 2, ahead).start()

        @pl.when(late(u))
        def _():
            far = genome(2, 0)
            y_copy(u, 0, 2, far, half=True).wait_recv()
            y_copy(u, 1, 2, far, half=True).wait_recv()
            x_copy(u, 3, far).start()

    def settle(u):
        @pl.when(jnp.logical_not(late(u)))
        def _():
            y_copy(u, 0, 1, genome(-1, 1)).wait_recv()
            y_copy(u, 1, 0, genome(1, 0)).wait_recv()
            y_copy(u, 0, 2, genome(-2, 0)).wait_recv()
            y_copy(u, 1, 2, genome(2, 1)).wait_recv()

        @pl.when(late(u))
        def _():
            x_copy(u, 0, genome(0, 1)).wait_recv()
            x_copy(u, 1, genome(-1, 1)).wait_recv()
            x_copy(u, 2, genome(1, 1)).wait_recv()
            x_copy(u, 3, genome(2, 1)).wait_recv()

    tile = min(256, acc.shape[1])

    def product(u, at):
        cols = pl.ds(pl.multiple_of(chip_at(u, -1) * 2 * BLK, 2 * BLK), 2 * BLK)
        return acc[:, at] + lax.dot_general(
            gath[u].reshape(WT * BLK, 2 * BLK),
            wout[at, cols],
            (((1,), (1,)), ((), ())),
            preferred_element_type=F32,
        )

    def project(u):
        settle(u)

        @pl.when(u == 0)
        def _():
            load_wout.wait()

        @pl.loop(0, acc.shape[1] // tile)
        def _(n):
            at = pl.ds(pl.multiple_of(n * tile, tile), tile)
            acc[:, at] = product(u, at)

    def embed():
        @pl.loop(1, WT)
        def _(d):
            whence = (wt - d + WT) % WT
            remote(
                tok_ref, tok_wt.at[whence], tw_send.at[d], tw_recv.at[d], wt_peer(d)
            ).wait_recv()

        @pl.loop(0, WT // 2)
        def _(g):
            hot = jnp.concatenate([one_hot(tok_wt[2 * g]), one_hot(tok_wt[2 * g + 1])], axis=0)
            acc[pl.ds(pl.multiple_of(g * 2 * BLK, 2 * BLK), 2 * BLK), :] = jnp.dot(
                hot, emb_ref[...], preferred_element_type=F32
            )

    stages = ((0, spread), (2, relay), (4, relay_again), (6, project))

    @pl.loop(0, nchip + stages[-1][0] - 1)
    def _(t):
        @pl.when(t < nchip // 2)
        def _():
            pl.loop(2 * t, 2 * t + 2)(mixer)

        for lag, stage in stages:

            @pl.when((t >= lag) & (t < nchip + lag))
            def _():
                stage(t - lag)

        pl.when(t == 2)(embed)

    last = nchip - 1
    settle(last)

    @pl.loop(0, acc.shape[1] // tile)
    def _(n):
        at = pl.ds(pl.multiple_of(n * tile, tile), tile)
        out_ref[:, :, at] = product(last, at).astype(BF16).reshape(WT, BLK, tile)

    @pl.loop(1, WT)
    def _(d):
        sq_copy(d).wait_send()
        part_copy(d).wait_send()
        tok_wt_copy(d).wait_send()
        vocab_copy(d).wait_send()

    @pl.loop(1, nseq)
    def _(d):
        tok_seq_copy(d).wait_send()

    @pl.loop(0, nchip)
    def _(u):
        for i in range(2):

            @pl.when(jnp.logical_not((u == 0) & (core == i)))
            def _():
                block_send(u, i).wait_send()

        x_copy(u, 0, wt).wait_send()
        for way in range(2):
            y_copy(u, way, 0, wt).wait_send()

        @pl.when(jnp.logical_not(late(u)))
        def _():
            for way in range(2):
                y_copy(u, way, 1, wt).wait_send()
                y_copy(u, way, 2, wt).wait_send()

        @pl.when(late(u))
        def _():
            for way in range(2):
                y_copy(u, way, 2, wt, half=True).wait_send()
            for kind in range(1, 4):
                x_copy(u, kind, wt).wait_send()


def local(nseq, tokens, embed_table, norm_gain, w_in, short_taps, filters, w_out):
    vocab, feats = embed_table.shape
    nchip = nseq // 2
    wide = 3 * BLK
    dma = pltpu.SemaphoreType.DMA
    vmem = pl.BlockSpec(memory_space=pltpu.VMEM)
    return pl.pallas_call(
        functools.partial(block_kernel, nseq, feats * WT),
        out_shape=jax.ShapeDtypeStruct((WT, BLK, feats), BF16),
        in_specs=[vmem] * 6 + [pl.BlockSpec(memory_space=pltpu.HBM)],
        out_specs=vmem,
        scratch_shapes=[
            pltpu.VMEM(w_out.shape, BF16),
            pltpu.VMEM((WT, vocab // WT, wide), BF16),
            pltpu.VMEM((WT, vocab // WT, wide), BF16),
            pltpu.VMEM((1, vocab), F32),
            pltpu.VMEM((WT, 1, vocab), F32),
            pltpu.VMEM((WT, vocab // WT, wide), BF16),
            pltpu.VMEM((nseq, 1, BLK), jnp.int32),
            pltpu.VMEM((WT, 1, BLK), jnp.int32),
            pltpu.VMEM((BLK // GSZ * BLK, 2 * BLK), BF16),
            pltpu.VMEM((HALO + 3 * BLK, wide), F32),
            pltpu.VMEM((nchip, 2, BLK, BLK), BF16),
            pltpu.VMEM((nchip, WT, BLK, 2 * BLK), BF16),
            pltpu.VMEM((WT * BLK, feats), F32),
            dma,
            dma,
            dma((WT,)),
            dma((WT,)),
            dma((WT,)),
            dma((WT,)),
            dma((WT,)),
            dma((WT,)),
            dma((nseq,)),
            dma((nseq,)),
            dma((WT,)),
            dma((WT,)),
            dma((nchip, 2)),
            dma((nchip, 2)),
            dma((nchip * 4,)),
            dma((nchip * 4,)),
            dma((nchip * 6,)),
            dma((nchip * 6,)),
        ],
        compiler_params=pltpu.CompilerParams(
            collective_id=0, has_side_effects=True, vmem_limit_bytes=50 * 2**20
        ),
        name="hyena_block",
    )(
        tokens,
        embed_table,
        norm_gain,
        jnp.transpose(w_in, (1, 0, 2)),
        short_taps,
        filters,
        w_out,
    )


def solution(mesh):
    placed = (
        P("wt", "seq"),
        P(None, "wt"),
        P("wt"),
        P("wt", None, "seq"),
        P(None, None, "seq"),
        P("seq", None),
        P("wt", None),
    )
    return jax.shard_map(
        functools.partial(local, mesh.shape["seq"]),
        mesh=mesh,
        in_specs=placed,
        out_specs=P(None, "seq", "wt"),
        check_vma=False,
    )
```

```python
import functools

import jax
import jax.numpy as jnp
from jax import lax
from jax.experimental import pallas as pl
from jax.experimental.pallas import tpu as pltpu
from jax.sharding import PartitionSpec as P

F32 = jnp.float32
BF16 = jnp.bfloat16
BLK = 128
GSZ = 16
HALO = 16
RING = 4
WT = 2 * RING


def block_kernel(
    nseq,
    feature_count,
    tok_ref,
    emb_ref,
    gain_ref,
    win_ref,
    taps_ref,
    filt_ref,
    wout_hbm,
    out_ref,
    wout,
    part_out,
    part_in,
    sq_out,
    sq_in,
    vtab,
    tok_seq,
    tok_wt,
    toep,
    ext,
    sbuf,
    gath,
    acc,
    wout_sem,
    self_sem,
    p_send,
    p_recv,
    q_send,
    q_recv,
    v_send,
    v_recv,
    ts_send,
    ts_recv,
    tw_send,
    tw_recv,
    s1,
    r1,
    sx,
    rx,
    sy,
    ry,
):
    nchip, nz = nseq // 2, nseq // 4
    seq = lax.axis_index("seq")
    wt = lax.axis_index("wt")
    chip, core = seq // 2, seq % 2
    y, xh = wt // 2, wt % 2
    vocab = emb_ref.shape[0]
    vrow = vocab // WT
    wide = 3 * BLK

    def genome(dy, flip):
        return ((y + dy + RING) % RING) * 2 + (xh if flip == 0 else 1 - xh)

    def remote(src, dst, ssem, rsem, where):
        return pltpu.make_async_remote_copy(
            src_ref=src,
            dst_ref=dst,
            send_sem=ssem,
            recv_sem=rsem,
            device_id=where,
            device_id_type=pl.DeviceIdType.MESH,
        )

    def seq_peer(d):
        return {"seq": (seq + d) % nseq}

    def wt_peer(d):
        return {"wt": (wt + d) % WT}

    barrier = pltpu.get_barrier_semaphore()

    @pl.loop(1, nseq)
    def _(d):
        pl.semaphore_signal(
            barrier, inc=1, device_id=seq_peer(d), device_id_type=pl.DeviceIdType.MESH
        )

    @pl.loop(1, WT)
    def _(d):
        pl.semaphore_signal(
            barrier, inc=1, device_id=wt_peer(d), device_id_type=pl.DeviceIdType.MESH
        )

    @pl.loop(0, nseq // 2)
    def _(k):
        across = {"seq": (1 - chip // nz) * (nseq // 2) + k, "wt": genome(0, 1)}
        pl.semaphore_signal(
            barrier, inc=1, device_id=across, device_id_type=pl.DeviceIdType.MESH
        )

    load_wout = pltpu.make_async_copy(wout_hbm, wout, wout_sem)
    load_wout.start()

    sq_out[...] = jnp.zeros_like(sq_out)
    rows = vocab // 2

    @pl.loop(0, 2)
    def _(i):
        e = emb_ref[pl.ds(pl.multiple_of(i * rows, rows), rows), :].astype(F32)
        sq = jnp.sum(e * e, axis=1, keepdims=True)
        r = lax.broadcasted_iota(jnp.int32, (rows, vocab), 0) + i * rows
        l = lax.broadcasted_iota(jnp.int32, (rows, vocab), 1)
        sq_out[...] += jnp.sum(jnp.where(r == l, sq, 0.0), axis=0, keepdims=True)
        gained = (e * gain_ref[...].astype(F32).reshape(1, -1)).astype(BF16)
        streams = jnp.concatenate([win_ref[k] for k in range(3)], axis=1)
        p = jnp.dot(gained, streams, preferred_element_type=F32).astype(BF16)
        for k in range(WT // 2):
            part_out[i * (WT // 2) + k] = p[k * vrow : (k + 1) * vrow]

    filt = filt_ref[...].astype(F32)
    for q in range(BLK // GSZ):
        row = jnp.concatenate([filt[q : q + 1], jnp.zeros((1, BLK), F32)], axis=1)
        rolled = pltpu.roll(
            jnp.broadcast_to(row, (2 * BLK, 2 * BLK)), BLK, 1, stride=1, stride_axis=0
        )
        toep[q * BLK : (q + 1) * BLK, :] = rolled[:, :BLK].T.astype(BF16)

    tok_seq[seq] = tok_ref[...]
    tok_wt[wt] = tok_ref[...]

    pl.semaphore_wait(barrier, nseq - 1 + WT - 1 + nseq // 2)

    def part_copy(d):
        return remote(
            part_out.at[(wt + d) % WT], part_in.at[d], p_send.at[d], p_recv.at[d], wt_peer(d)
        )

    def sq_copy(d):
        return remote(sq_out, sq_in.at[d], q_send.at[d], q_recv.at[d], wt_peer(d))

    def tok_wt_copy(d):
        return remote(tok_ref, tok_wt.at[wt], tw_send.at[d], tw_recv.at[d], wt_peer(d))

    def tok_seq_copy(d):
        return remote(tok_ref, tok_seq.at[seq], ts_send.at[d], ts_recv.at[d], seq_peer(d))

    @pl.loop(1, WT)
    def _(d):
        sq_copy(d).start()
        part_copy(d).start()

    @pl.loop(1, WT)
    def _(d):
        tok_wt_copy(d).start()

    @pl.loop(1, nseq)
    def _(d):
        tok_seq_copy(d).start()

    @pl.loop(1, WT)
    def _(d):
        sq_copy(d).wait_recv()
        part_copy(d).wait_recv()

    total = part_out[wt].astype(F32)
    squares = sq_out[...]
    for d in range(1, WT):
        total = total + part_in[d].astype(F32)
        squares = squares + sq_in[d]
    scale = lax.rsqrt(squares / feature_count + 1e-06)
    r = lax.broadcasted_iota(jnp.int32, (vrow, vocab), 0) + wt * vrow
    l = lax.broadcasted_iota(jnp.int32, (vrow, vocab), 1)
    scale_col = jnp.sum(jnp.where(r == l, scale, 0.0), axis=1, keepdims=True)
    vtab[wt] = (total * scale_col).astype(BF16)

    def vocab_copy(d):
        return remote(vtab.at[wt], vtab.at[wt], v_send.at[d], v_recv.at[d], wt_peer(d))

    def vocab_arrival(d):
        whence = (wt - d + WT) % WT
        return remote(
            vtab.at[whence], vtab.at[whence], v_send.at[d], v_recv.at[d], wt_peer(d)
        )

    @pl.loop(1, WT)
    def _(d):
        vocab_copy(d).start()

    def one_hot(row):
        cols = jnp.broadcast_to(row, (BLK, BLK)).T
        lane = lax.broadcasted_iota(jnp.int32, (BLK, BLK), 1)
        return jnp.concatenate(
            [
                jnp.where(cols == lane + k * BLK, 1.0, 0.0).astype(BF16)
                for k in range(vocab // BLK)
            ],
            axis=1,
        )

    @pl.loop(1, WT)
    def _(d):
        whence = (wt - d + WT) % WT
        remote(
            tok_ref, tok_wt.at[whence], tw_send.at[d], tw_recv.at[d], wt_peer(d)
        ).wait_recv()

    @pl.loop(0, WT // 2)
    def _(g):
        hot = jnp.concatenate([one_hot(tok_wt[2 * g]), one_hot(tok_wt[2 * g + 1])], axis=0)
        acc[pl.ds(pl.multiple_of(g * 2 * BLK, 2 * BLK), 2 * BLK), :] = jnp.dot(
            hot, emb_ref[...], preferred_element_type=F32
        )

    @pl.loop(1, nseq)
    def _(d):
        whence = (seq - d + nseq) % nseq
        remote(
            tok_ref, tok_seq.at[whence], ts_send.at[d], ts_recv.at[d], seq_peer(d)
        ).wait_recv()

    @pl.loop(1, WT)
    def _(d):
        vocab_arrival(d).wait_recv()

    def pick(u, values):
        return sum((jnp.where(u == k, v, 0) for k, v in enumerate(values) if v), 0)

    steps = [0, 1, -1, 2, -2, 3, -3, 4] if nz == 8 else list(range(nz))
    order = [(flip, step) for step in steps for flip in range(2)]
    flips = [flip for flip, _ in order]

    def offset(u):
        return pick(u, flips), pick(u, [step for _, step in order])

    def direct(u):
        return pick(u, flips) == 1

    def late(u):
        return (pick(u, flips) == 0) & (u > 0)

    def crossing(u):
        return u == 0

    def chip_at(u, sign):
        flip, step = offset(u)
        xl, z = chip // nz, chip % nz
        return ((xl + flip) % 2) * nz + (z + sign * step + nz) % nz

    def pick(u, values):
        return sum((jnp.where(u == k, v, 0) for k, v in enumerate(values) if v), 0)

    steps = [0, 1, -1, 2, -2, 3, -3, 4] if nz == 8 else list(range(nz))
    order = [(flip, step) for step in steps for flip in range(2)]
    flips = [flip for flip, _ in order]

    def offset(u):
        return pick(u, flips), pick(u, [step for _, step in order])

    def direct(u):
        return pick(u, flips) == 1

    def late(u):
        return (pick(u, flips) == 0) & (u > 0)

    def crossing(u):
        return u == 0

    def chip_at(u, sign):
        flip, step = offset(u)
        xl, z = chip // nz, chip % nz
        return ((xl + flip) % 2) * nz + (z + sign * step + nz) % nz

    def block_send(u, i):
        to = 2 * chip_at(u, 1) + i
        return remote(
            sbuf.at[u, i],
            gath.at[u, wt, core],
            s1.at[u, i],
            r1.at[u, core],
            {"seq": to},
        )

    def block_local(i):
        return pltpu.make_async_copy(
            sbuf.at[0, i],
            gath.at[0, wt, core],
            self_sem,
        )

    def block_arrival(u, i):
        return remote(
            sbuf.at[u, i],
            gath.at[u, wt, i],
            s1.at[u, i],
            r1.at[u, i],
            {"seq": 2 * chip_at(u, 1) + i},
        )

    def block_send(u, i, twin=0):
        return remote(
            sbuf.at[u, i],
            gath.at[u, wt, core],
            s1.at[u, 2 * twin + i],
            r1.at[u, 2 * twin + core],
            {"seq": 2 * chip_at(u, 1) + i, "wt": genome(0, twin)},
        )

    def block_local(i):
        return pltpu.make_async_copy(
            sbuf.at[0, i],
            gath.at[0, wt, core],
            self_sem,
        )

    def block_arrival(u, i, twin=0):
        return remote(
            sbuf.at[u, i],
            gath.at[u, genome(0, twin), i],
            s1.at[u, 2 * twin + i],
            r1.at[u, 2 * twin + i],
            {"seq": 2 * chip_at(u, 1) + i, "wt": genome(0, twin)},
        )

    def mixer(u):
        at = chip_at(u, 1)
        before = (2 * at - 2 + nseq) % nseq
        hot = jnp.concatenate(
            [one_hot(tok_seq[before])[BLK - HALO :]]
            + [one_hot(tok_seq[(before + k) % nseq]) for k in range(1, 4)],
            axis=0,
        )
        proj = jnp.dot(hot, vtab[...].reshape(vocab, wide), preferred_element_type=F32)
        past = HALO + BLK
        ext[:past, :] = jnp.where(at > 0, proj[:past], 0.0)
        ext[past:, :] = proj[past:]

        def mixed(s, start, rows):
            lanes = slice(s * BLK, (s + 1) * BLK)
            return sum(
                taps_ref[k][s : s + 1].astype(F32) * ext[start - k : start - k + rows, lanes]
                for k in range(3)
            )

        inner = (mixed(0, HALO, 3 * BLK) * mixed(2, HALO, 3 * BLK)).astype(BF16)
        middle = mixed(1, past, 2 * BLK)
        prior, first, second = (inner[k * BLK : (k + 1) * BLK] for k in range(3))
        pair = jnp.concatenate(
            [
                jnp.concatenate([prior, first], axis=1),
                jnp.concatenate([first, second], axis=1),
            ],
            axis=0,
        )
        filtered = jnp.dot(toep[...], pair, preferred_element_type=F32)
        group = (lax.broadcasted_iota(jnp.int32, (BLK, 2 * BLK), 1) % BLK) // GSZ
        conv = filtered[0:BLK]
        for q in range(1, BLK // GSZ):
            conv = jnp.where(group == q, filtered[q * BLK : (q + 1) * BLK], conv)
        sbuf[u, 0] = (middle[:BLK] * conv[:, :BLK]).astype(BF16)
        sbuf[u, 1] = (middle[BLK:] * conv[:, BLK:]).astype(BF16)
        for i in range(2):
            mine = (u == 0) & (core == i)

            @pl.when(mine)
            def _():
                block_local(i).start()

            @pl.when(jnp.logical_not(mine))
            def _():
                block_send(u, i).start()

            @pl.when(direct(u))
            def _():
                block_send(u, i, 1).start()

    def x_copy(u, kind, g):
        k = u * 4 + kind
        return remote(
            gath.at[u, g], gath.at[u, g], sx.at[k], rx.at[k], {"wt": genome(0, 1)}
        )

    def y_copy(u, way, kind, g, half=False):
        k = (u * 2 + way) * 3 + kind
        to = genome(1 if way == 0 else -1, 0)
        part = gath.at[u, g]
        if half:
            part = gath.at[u, g, way]
        return remote(part, part, sy.at[k], ry.at[k], {"wt": to})

    def spread(u):
        for i in range(2):
            mine = (u == 0) & (core == i)

            @pl.when(mine)
            def _():
                block_local(i).wait()

            @pl.when(jnp.logical_not(mine))
            def _():
                block_arrival(u, i).wait_recv()

        y_copy(u, 0, 0, wt).start()
        y_copy(u, 1, 0, wt).start()

        @pl.when(jnp.logical_not(direct(u)))
        def _():
            x_copy(u, 0, wt).start()

        @pl.when(direct(u))
        def _():
            other = genome(0, 1)
            for i in range(2):
                block_arrival(u, i, 1).wait_recv()
            y_copy(u, 0, 1, other).start()
            y_copy(u, 1, 1, other).start()

    def relay(u):
        @pl.when(crossing(u))
        def _():
            other = genome(0, 1)
            x_copy(u, 0, other).wait_recv()
            y_copy(u, 0, 1, other).start()
            y_copy(u, 1, 1, other).start()

        @pl.when(late(u))
        def _():
            for way, dy in ((0, -1), (1, 1)):
                g = genome(dy, 0)
                y_copy(u, way, 0, g).wait_recv()
                y_copy(u, way, 2, g, half=True).start()
                x_copy(u, 1 + way, g).start()

    def relay_again(u):
        @pl.when(jnp.logical_not(late(u)))
        def _():
            behind = genome(-1, 0)
            y_copy(u, 0, 0, behind).wait_recv()
            y_copy(u, 0, 2, behind).start()
            ahead = genome(1, 1)
            y_copy(u, 1, 1, ahead).wait_recv()
            y_copy(u, 1, 2, ahead).start()

        @pl.when(late(u))
        def _():
            far = genome(2, 0)
            y_copy(u, 0, 2, far, half=True).wait_recv()
            y_copy(u, 1, 2, far, half=True).wait_recv()
            x_copy(u, 3, far).start()

    def settle(u):
        @pl.when(jnp.logical_not(late(u)))
        def _():
            y_copy(u, 0, 1, genome(-1, 1)).wait_recv()
            y_copy(u, 1, 0, genome(1, 0)).wait_recv()
            y_copy(u, 0, 2, genome(-2, 0)).wait_recv()
            y_copy(u, 1, 2, genome(2, 1)).wait_recv()

        @pl.when(late(u))
        def _():
            x_copy(u, 0, genome(0, 1)).wait_recv()
            x_copy(u, 1, genome(-1, 1)).wait_recv()
            x_copy(u, 2, genome(1, 1)).wait_recv()
            x_copy(u, 3, genome(2, 1)).wait_recv()

    tile = min(256, acc.shape[1])

    def product(u, at):
        cols = pl.ds(pl.multiple_of(chip_at(u, -1) * 2 * BLK, 2 * BLK), 2 * BLK)
        return acc[:, at] + lax.dot_general(
            jnp.concatenate(
                [gath[u, :, i].reshape(WT * BLK, BLK) for i in range(2)], axis=1
            ),
            wout[at, cols],
            (((1,), (1,)), ((), ())),
            preferred_element_type=F32,
        )

    def project(u):
        settle(u)

        @pl.when(u == 0)
        def _():
            load_wout.wait()

        @pl.loop(0, acc.shape[1] // tile)
        def _(n):
            at = pl.ds(pl.multiple_of(n * tile, tile), tile)
            acc[:, at] = product(u, at)

    stages = ((0, spread), (2, relay), (4, relay_again), (6, project))

    @pl.loop(0, nchip + stages[-1][0] - 1)
    def _(t):
        def mixed(t):
            return jnp.minimum(jnp.minimum(2 * t + 2, t + 5), nchip)

        pl.loop(mixed(t - 1), mixed(t))(mixer)

        for lag, stage in stages:

            @pl.when((t >= lag) & (t < nchip + lag))
            def _():
                stage(t - lag)

    last = nchip - 1
    settle(last)

    @pl.loop(0, acc.shape[1] // tile)
    def _(n):
        at = pl.ds(pl.multiple_of(n * tile, tile), tile)
        out_ref[:, :, at] = product(last, at).astype(BF16).reshape(WT, BLK, tile)

    @pl.loop(1, WT)
    def _(d):
        sq_copy(d).wait_send()
        part_copy(d).wait_send()
        tok_wt_copy(d).wait_send()
        vocab_copy(d).wait_send()

    @pl.loop(1, nseq)
    def _(d):
        tok_seq_copy(d).wait_send()

    @pl.loop(0, nchip)
    def _(u):
        for i in range(2):

            @pl.when(jnp.logical_not((u == 0) & (core == i)))
            def _():
                block_send(u, i).wait_send()

            @pl.when(direct(u))
            def _():
                block_send(u, i, 1).wait_send()

        @pl.when(jnp.logical_not(direct(u)))
        def _():
            x_copy(u, 0, wt).wait_send()

        for way in range(2):
            y_copy(u, way, 0, wt).wait_send()

        @pl.when(jnp.logical_not(late(u)))
        def _():
            for way in range(2):
                y_copy(u, way, 1, wt).wait_send()
                y_copy(u, way, 2, wt).wait_send()

        @pl.when(late(u))
        def _():
            for way in range(2):
                y_copy(u, way, 2, wt, half=True).wait_send()
            for kind in range(1, 4):
                x_copy(u, kind, wt).wait_send()


def local(nseq, tokens, embed_table, norm_gain, w_in, short_taps, filters, w_out):
    vocab, feats = embed_table.shape
    nchip = nseq // 2
    wide = 3 * BLK
    dma = pltpu.SemaphoreType.DMA
    vmem = pl.BlockSpec(memory_space=pltpu.VMEM)
    return pl.pallas_call(
        functools.partial(block_kernel, nseq, feats * WT),
        out_shape=jax.ShapeDtypeStruct((WT, BLK, feats), BF16),
        in_specs=[vmem] * 6 + [pl.BlockSpec(memory_space=pltpu.HBM)],
        out_specs=vmem,
        scratch_shapes=[
            pltpu.VMEM(w_out.shape, BF16),
            pltpu.VMEM((WT, vocab // WT, wide), BF16),
            pltpu.VMEM((WT, vocab // WT, wide), BF16),
            pltpu.VMEM((1, vocab), F32),
            pltpu.VMEM((WT, 1, vocab), F32),
            pltpu.VMEM((WT, vocab // WT, wide), BF16),
            pltpu.VMEM((nseq, 1, BLK), jnp.int32),
            pltpu.VMEM((WT, 1, BLK), jnp.int32),
            pltpu.VMEM((BLK // GSZ * BLK, 2 * BLK), BF16),
            pltpu.VMEM((HALO + 3 * BLK, wide), F32),
            pltpu.VMEM((nchip, 2, BLK, BLK), BF16),
            pltpu.VMEM((nchip, WT, 2, BLK, BLK), BF16),
            pltpu.VMEM((WT * BLK, feats), F32),
            dma,
            dma,
            dma((WT,)),
            dma((WT,)),
            dma((WT,)),
            dma((WT,)),
            dma((WT,)),
            dma((WT,)),
            dma((nseq,)),
            dma((nseq,)),
            dma((WT,)),
            dma((WT,)),
            dma((nchip, 4)),
            dma((nchip, 4)),
            dma((nchip * 4,)),
            dma((nchip * 4,)),
            dma((nchip * 6,)),
            dma((nchip * 6,)),
        ],
        compiler_params=pltpu.CompilerParams(
            collective_id=0, has_side_effects=True, vmem_limit_bytes=50 * 2**20
        ),
        name="hyena_block",
    )(
        *(
            pltpu.with_memory_space_constraint(x, pltpu.HBM)
            for x in (
                tokens,
                embed_table,
                norm_gain,
                jnp.transpose(w_in, (1, 0, 2)),
                short_taps,
                filters,
                w_out,
            )
        )
    )


def solution(mesh):
    placed = (
        P("wt", "seq"),
        P(None, "wt"),
        P("wt"),
        P("wt", None, "seq"),
        P(None, None, "seq"),
        P("seq", None),
        P("wt", None),
    )
    return jax.shard_map(
        functools.partial(local, mesh.shape["seq"]),
        mesh=mesh,
        in_specs=placed,
        out_specs=P(None, "seq", "wt"),
        check_vma=False,
    )
```

```python
import functools

import jax
import jax.numpy as jnp
from jax import lax
from jax.experimental import pallas as pl
from jax.experimental.pallas import tpu as pltpu
from jax.sharding import PartitionSpec as P

F32 = jnp.float32
BF16 = jnp.bfloat16
BLK = 128
GSZ = 16
HALO = 16
RING = 4
WT = 2 * RING


def block_kernel(
    nseq,
    feature_count,
    tok_ref,
    emb_ref,
    gain_ref,
    win_ref,
    taps_ref,
    filt_ref,
    wout_hbm,
    out_ref,
    wout,
    part_out,
    part_in,
    sq_out,
    sq_in,
    vtab,
    tok_seq,
    tok_wt,
    toep,
    ext,
    sbuf,
    gath,
    acc,
    wout_sem,
    self_sem,
    p_send,
    p_recv,
    q_send,
    q_recv,
    v_send,
    v_recv,
    ts_send,
    ts_recv,
    tw_send,
    tw_recv,
    s1,
    r1,
    sx,
    rx,
    sy,
    ry,
):
    nchip, nz = nseq // 2, nseq // 4
    seq = lax.axis_index("seq")
    wt = lax.axis_index("wt")
    chip, core = seq // 2, seq % 2
    y, xh = wt // 2, wt % 2
    vocab = emb_ref.shape[0]
    vrow = vocab // WT
    half = vrow // 2
    wide = 3 * BLK

    def genome(dy, flip):
        return ((y + dy + RING) % RING) * 2 + (xh if flip == 0 else 1 - xh)

    def remote(src, dst, ssem, rsem, where):
        return pltpu.make_async_remote_copy(
            src_ref=src,
            dst_ref=dst,
            send_sem=ssem,
            recv_sem=rsem,
            device_id=where,
            device_id_type=pl.DeviceIdType.MESH,
        )

    def seq_peer(d):
        return {"seq": (seq + d) % nseq}

    def wt_peer(d):
        return {"wt": (wt + d) % WT}

    barrier = pltpu.get_barrier_semaphore()

    @pl.loop(1, nseq)
    def _(d):
        pl.semaphore_signal(
            barrier, inc=1, device_id=seq_peer(d), device_id_type=pl.DeviceIdType.MESH
        )

    @pl.loop(1, WT)
    def _(d):
        pl.semaphore_signal(
            barrier, inc=1, device_id=wt_peer(d), device_id_type=pl.DeviceIdType.MESH
        )

    @pl.loop(0, nseq // 2)
    def _(k):
        across = {"seq": (1 - chip // nz) * (nseq // 2) + k, "wt": genome(0, 1)}
        pl.semaphore_signal(
            barrier, inc=1, device_id=across, device_id_type=pl.DeviceIdType.MESH
        )

    load_wout = pltpu.make_async_copy(wout_hbm, wout, wout_sem)
    load_wout.start()

    sq_out[...] = jnp.zeros_like(sq_out)
    rows = vocab // 2

    @pl.loop(0, 2)
    def _(i):
        e = emb_ref[pl.ds(pl.multiple_of(i * rows, rows), rows), :].astype(F32)
        sq = jnp.sum(e * e, axis=1, keepdims=True)
        r = lax.broadcasted_iota(jnp.int32, (rows, vocab), 0) + i * rows
        l = lax.broadcasted_iota(jnp.int32, (rows, vocab), 1)
        sq_out[...] += jnp.sum(jnp.where(r == l, sq, 0.0), axis=0, keepdims=True)
        gained = (e * gain_ref[...].astype(F32).reshape(1, -1)).astype(BF16)
        streams = jnp.concatenate([win_ref[k] for k in range(3)], axis=1)
        p = jnp.dot(gained, streams, preferred_element_type=F32).astype(BF16)
        for k in range(WT // 2):
            part_out[i * (WT // 2) + k] = p[k * vrow : (k + 1) * vrow].reshape(2, half, wide)

    filt = filt_ref[...].astype(F32)
    for q in range(BLK // GSZ):
        row = jnp.concatenate([filt[q : q + 1], jnp.zeros((1, BLK), F32)], axis=1)
        rolled = pltpu.roll(
            jnp.broadcast_to(row, (2 * BLK, 2 * BLK)), BLK, 1, stride=1, stride_axis=0
        )
        toep[q * BLK : (q + 1) * BLK, :] = rolled[:, :BLK].T.astype(BF16)

    tok_seq[seq] = tok_ref[...]
    tok_wt[wt] = tok_ref[...]

    pl.semaphore_wait(barrier, nseq - 1 + WT - 1 + nseq // 2)

    def part_copy(d, h):
        return remote(
            part_out.at[(wt + d) % WT, h],
            part_in.at[d, h],
            p_send.at[h, d],
            p_recv.at[h, d],
            wt_peer(d),
        )

    def sq_copy(d):
        return remote(sq_out, sq_in.at[d], q_send.at[d], q_recv.at[d], wt_peer(d))

    def tok_wt_copy(d):
        return remote(tok_ref, tok_wt.at[wt], tw_send.at[d], tw_recv.at[d], wt_peer(d))

    def tok_seq_copy(d):
        return remote(tok_ref, tok_seq.at[seq], ts_send.at[d], ts_recv.at[d], seq_peer(d))

    @pl.loop(1, WT)
    def _(d):
        sq_copy(d).start()
        part_copy(d, 0).start()

    @pl.loop(1, WT)
    def _(d):
        part_copy(d, 1).start()

    @pl.loop(1, WT)
    def _(d):
        tok_wt_copy(d).start()

    @pl.loop(1, nseq)
    def _(d):
        tok_seq_copy(d).start()

    def vocab_copy(d, h):
        return remote(
            vtab.at[wt, h], vtab.at[wt, h], v_send.at[h, d], v_recv.at[h, d], wt_peer(d)
        )

    def vocab_arrival(d, h):
        whence = (wt - d + WT) % WT
        return remote(
            vtab.at[whence, h], vtab.at[whence, h], v_send.at[h, d], v_recv.at[h, d], wt_peer(d)
        )

    @pl.loop(1, WT)
    def _(d):
        sq_copy(d).wait_recv()

    squares = sq_out[...]
    for d in range(1, WT):
        squares = squares + sq_in[d]
    scale = lax.rsqrt(squares / feature_count + 1e-06)
    for h in range(2):

        @pl.loop(1, WT)
        def _(d):
            part_copy(d, h).wait_recv()

        total = part_out[wt, h].astype(F32)
        for d in range(1, WT):
            total = total + part_in[d, h].astype(F32)
        r = lax.broadcasted_iota(jnp.int32, (half, vocab), 0) + wt * vrow + h * half
        l = lax.broadcasted_iota(jnp.int32, (half, vocab), 1)
        scale_col = jnp.sum(jnp.where(r == l, scale, 0.0), axis=1, keepdims=True)
        vtab[wt, h] = (total * scale_col).astype(BF16)

        @pl.loop(1, WT)
        def _(d):
            vocab_copy(d, h).start()

    def one_hot(row):
        cols = jnp.broadcast_to(row, (BLK, BLK)).T
        lane = lax.broadcasted_iota(jnp.int32, (BLK, BLK), 1)
        return jnp.concatenate(
            [
                jnp.where(cols == lane + k * BLK, 1.0, 0.0).astype(BF16)
                for k in range(vocab // BLK)
            ],
            axis=1,
        )

    @pl.loop(1, WT)
    def _(d):
        whence = (wt - d + WT) % WT
        remote(
            tok_ref, tok_wt.at[whence], tw_send.at[d], tw_recv.at[d], wt_peer(d)
        ).wait_recv()

    @pl.loop(0, WT // 2)
    def _(g):
        hot = jnp.concatenate([one_hot(tok_wt[2 * g]), one_hot(tok_wt[2 * g + 1])], axis=0)
        acc[pl.ds(pl.multiple_of(g * 2 * BLK, 2 * BLK), 2 * BLK), :] = jnp.dot(
            hot, emb_ref[...], preferred_element_type=F32
        )

    @pl.loop(1, nseq)
    def _(d):
        whence = (seq - d + nseq) % nseq
        remote(
            tok_ref, tok_seq.at[whence], ts_send.at[d], ts_recv.at[d], seq_peer(d)
        ).wait_recv()

    @pl.loop(1, WT)
    def _(d):
        for h in range(2):
            vocab_arrival(d, h).wait_recv()

    def pick(u, values):
        return sum((jnp.where(u == k, v, 0) for k, v in enumerate(values) if v), 0)

    steps = [0, 1, -1, 2, -2, 3, -3, 4] if nz == 8 else list(range(nz))
    order = [(flip, step) for step in steps for flip in range(2)]
    flips = [flip for flip, _ in order]

    def offset(u):
        return pick(u, flips), pick(u, [step for _, step in order])

    def direct(u):
        return pick(u, flips) == 1

    def late(u):
        return (pick(u, flips) == 0) & (u > 0)

    def crossing(u):
        return u == 0

    def chip_at(u, sign):
        flip, step = offset(u)
        xl, z = chip // nz, chip % nz
        return ((xl + flip) % 2) * nz + (z + sign * step + nz) % nz

    def pick(u, values):
        return sum((jnp.where(u == k, v, 0) for k, v in enumerate(values) if v), 0)

    steps = [0, 1, -1, 2, -2, 3, -3, 4] if nz == 8 else list(range(nz))
    order = [(flip, step) for step in steps for flip in range(2)]
    flips = [flip for flip, _ in order]

    def offset(u):
        return pick(u, flips), pick(u, [step for _, step in order])

    def direct(u):
        return pick(u, flips) == 1

    def late(u):
        return (pick(u, flips) == 0) & (u > 0)

    def crossing(u):
        return u == 0

    def chip_at(u, sign):
        flip, step = offset(u)
        xl, z = chip // nz, chip % nz
        return ((xl + flip) % 2) * nz + (z + sign * step + nz) % nz

    def block_send(u, i):
        to = 2 * chip_at(u, 1) + i
        return remote(
            sbuf.at[u, i],
            gath.at[u, wt, core],
            s1.at[u, i],
            r1.at[u, core],
            {"seq": to},
        )

    def block_local(i):
        return pltpu.make_async_copy(
            sbuf.at[0, i],
            gath.at[0, wt, core],
            self_sem,
        )

    def block_arrival(u, i):
        return remote(
            sbuf.at[u, i],
            gath.at[u, wt, i],
            s1.at[u, i],
            r1.at[u, i],
            {"seq": 2 * chip_at(u, 1) + i},
        )

    def block_send(u, i, twin=0):
        return remote(
            sbuf.at[u, i],
            gath.at[u, wt, core],
            s1.at[u, 2 * twin + i],
            r1.at[u, 2 * twin + core],
            {"seq": 2 * chip_at(u, 1) + i, "wt": genome(0, twin)},
        )

    def block_local(i):
        return pltpu.make_async_copy(
            sbuf.at[0, i],
            gath.at[0, wt, core],
            self_sem,
        )

    def block_arrival(u, i, twin=0):
        return remote(
            sbuf.at[u, i],
            gath.at[u, genome(0, twin), i],
            s1.at[u, 2 * twin + i],
            r1.at[u, 2 * twin + i],
            {"seq": 2 * chip_at(u, 1) + i, "wt": genome(0, twin)},
        )

    def mixer(u):
        at = chip_at(u, 1)
        before = (2 * at - 2 + nseq) % nseq
        hot = jnp.concatenate(
            [one_hot(tok_seq[before])[BLK - HALO :]]
            + [one_hot(tok_seq[(before + k) % nseq]) for k in range(1, 4)],
            axis=0,
        )
        proj = jnp.dot(hot, vtab[...].reshape(vocab, wide), preferred_element_type=F32)
        past = HALO + BLK
        ext[:past, :] = jnp.where(at > 0, proj[:past], 0.0)
        ext[past:, :] = proj[past:]

        def mixed(s, start, rows):
            lanes = slice(s * BLK, (s + 1) * BLK)
            return sum(
                taps_ref[k][s : s + 1].astype(F32) * ext[start - k : start - k + rows, lanes]
                for k in range(3)
            )

        inner = (mixed(0, HALO, 3 * BLK) * mixed(2, HALO, 3 * BLK)).astype(BF16)
        middle = mixed(1, past, 2 * BLK)
        prior, first, second = (inner[k * BLK : (k + 1) * BLK] for k in range(3))
        pair = jnp.concatenate(
            [
                jnp.concatenate([prior, first], axis=1),
                jnp.concatenate([first, second], axis=1),
            ],
            axis=0,
        )
        filtered = jnp.dot(toep[...], pair, preferred_element_type=F32)
        group = (lax.broadcasted_iota(jnp.int32, (BLK, 2 * BLK), 1) % BLK) // GSZ
        conv = filtered[0:BLK]
        for q in range(1, BLK // GSZ):
            conv = jnp.where(group == q, filtered[q * BLK : (q + 1) * BLK], conv)
        sbuf[u, 0] = (middle[:BLK] * conv[:, :BLK]).astype(BF16)
        sbuf[u, 1] = (middle[BLK:] * conv[:, BLK:]).astype(BF16)
        for i in range(2):
            mine = (u == 0) & (core == i)

            @pl.when(mine)
            def _():
                block_local(i).start()

            @pl.when(jnp.logical_not(mine))
            def _():
                block_send(u, i).start()

            @pl.when(direct(u))
            def _():
                block_send(u, i, 1).start()

    def x_copy(u, kind, g):
        k = u * 4 + kind
        return remote(
            gath.at[u, g], gath.at[u, g], sx.at[k], rx.at[k], {"wt": genome(0, 1)}
        )

    def y_copy(u, way, kind, g, half=False):
        k = (u * 2 + way) * 3 + kind
        to = genome(1 if way == 0 else -1, 0)
        part = gath.at[u, g]
        if half:
            part = gath.at[u, g, way]
        return remote(part, part, sy.at[k], ry.at[k], {"wt": to})

    def spread(u):
        for i in range(2):
            mine = (u == 0) & (core == i)

            @pl.when(mine)
            def _():
                block_local(i).wait()

            @pl.when(jnp.logical_not(mine))
            def _():
                block_arrival(u, i).wait_recv()

        y_copy(u, 0, 0, wt).start()
        y_copy(u, 1, 0, wt).start()

        @pl.when(jnp.logical_not(direct(u)))
        def _():
            x_copy(u, 0, wt).start()

        @pl.when(direct(u))
        def _():
            other = genome(0, 1)
            for i in range(2):
                block_arrival(u, i, 1).wait_recv()
            y_copy(u, 0, 1, other).start()
            y_copy(u, 1, 1, other).start()

    def relay(u):
        @pl.when(crossing(u))
        def _():
            other = genome(0, 1)
            x_copy(u, 0, other).wait_recv()
            y_copy(u, 0, 1, other).start()
            y_copy(u, 1, 1, other).start()

        @pl.when(late(u))
        def _():
            for way, dy in ((0, -1), (1, 1)):
                g = genome(dy, 0)
                y_copy(u, way, 0, g).wait_recv()
                y_copy(u, way, 2, g, half=True).start()
                x_copy(u, 1 + way, g).start()

    def relay_again(u):
        @pl.when(jnp.logical_not(late(u)))
        def _():
            behind = genome(-1, 0)
            y_copy(u, 0, 0, behind).wait_recv()
            y_copy(u, 0, 2, behind).start()
            ahead = genome(1, 1)
            y_copy(u, 1, 1, ahead).wait_recv()
            y_copy(u, 1, 2, ahead).start()

        @pl.when(late(u))
        def _():
            far = genome(2, 0)
            y_copy(u, 0, 2, far, half=True).wait_recv()
            y_copy(u, 1, 2, far, half=True).wait_recv()
            x_copy(u, 3, far).start()

    def settle(u):
        @pl.when(jnp.logical_not(late(u)))
        def _():
            y_copy(u, 0, 1, genome(-1, 1)).wait_recv()
            y_copy(u, 1, 0, genome(1, 0)).wait_recv()
            y_copy(u, 0, 2, genome(-2, 0)).wait_recv()
            y_copy(u, 1, 2, genome(2, 1)).wait_recv()

        @pl.when(late(u))
        def _():
            x_copy(u, 0, genome(0, 1)).wait_recv()
            x_copy(u, 1, genome(-1, 1)).wait_recv()
            x_copy(u, 2, genome(1, 1)).wait_recv()
            x_copy(u, 3, genome(2, 1)).wait_recv()

    tile = min(256, acc.shape[1])

    def product(units, at):
        held = [gath[u, :, i].reshape(WT * BLK, BLK) for u in units for i in range(2)]
        weights = [
            wout[at, pl.ds(pl.multiple_of(chip_at(u, -1) * 2 * BLK, 2 * BLK), 2 * BLK)]
            for u in units
        ]
        return acc[:, at] + lax.dot_general(
            jnp.concatenate(held, axis=1),
            jnp.concatenate(weights, axis=1),
            (((1,), (1,)), ((), ())),
            preferred_element_type=F32,
        )

    def project(units):
        for u in units:
            settle(u)

        @pl.loop(0, acc.shape[1] // tile)
        def _(n):
            at = pl.ds(pl.multiple_of(n * tile, tile), tile)
            acc[:, at] = product(units, at)

    def project_some(u):
        pl.when(u == 0)(load_wout.wait)

        @pl.when((u % 2 == 1) & (u < nchip - 1))
        def _():
            project((u - 1, u))

        @pl.when(u == nchip - 2)
        def _():
            project((u,))

    stages = ((0, spread), (2, relay), (4, relay_again), (8, project_some))

    @pl.loop(0, nchip + stages[-1][0] - 1)
    def _(t):
        def mixed(t):
            return jnp.minimum(jnp.minimum(2 * t + 2, t + 5), nchip)

        pl.loop(mixed(t - 1), mixed(t))(mixer)

        for lag, stage in stages:

            @pl.when((t >= lag) & (t < nchip + lag))
            def _():
                stage(t - lag)

    last = nchip - 1
    settle(last)

    @pl.loop(0, acc.shape[1] // tile)
    def _(n):
        at = pl.ds(pl.multiple_of(n * tile, tile), tile)
        out_ref[:, :, at] = product((last,), at).astype(BF16).reshape(WT, BLK, tile)

    @pl.loop(1, WT)
    def _(d):
        sq_copy(d).wait_send()
        for h in range(2):
            part_copy(d, h).wait_send()
            vocab_copy(d, h).wait_send()
        tok_wt_copy(d).wait_send()

    @pl.loop(1, nseq)
    def _(d):
        tok_seq_copy(d).wait_send()

    @pl.loop(0, nchip)
    def _(u):
        for i in range(2):

            @pl.when(jnp.logical_not((u == 0) & (core == i)))
            def _():
                block_send(u, i).wait_send()

            @pl.when(direct(u))
            def _():
                block_send(u, i, 1).wait_send()

        @pl.when(jnp.logical_not(direct(u)))
        def _():
            x_copy(u, 0, wt).wait_send()

        for way in range(2):
            y_copy(u, way, 0, wt).wait_send()

        @pl.when(jnp.logical_not(late(u)))
        def _():
            for way in range(2):
                y_copy(u, way, 1, wt).wait_send()
                y_copy(u, way, 2, wt).wait_send()

        @pl.when(late(u))
        def _():
            for way in range(2):
                y_copy(u, way, 2, wt, half=True).wait_send()
            for kind in range(1, 4):
                x_copy(u, kind, wt).wait_send()


def local(nseq, tokens, embed_table, norm_gain, w_in, short_taps, filters, w_out):
    vocab, feats = embed_table.shape
    nchip = nseq // 2
    wide = 3 * BLK
    dma = pltpu.SemaphoreType.DMA
    vmem = pl.BlockSpec(memory_space=pltpu.VMEM)
    return pl.pallas_call(
        functools.partial(block_kernel, nseq, feats * WT),
        out_shape=jax.ShapeDtypeStruct((WT, BLK, feats), BF16),
        in_specs=[vmem] * 6 + [pl.BlockSpec(memory_space=pltpu.HBM)],
        out_specs=vmem,
        scratch_shapes=[
            pltpu.VMEM(w_out.shape, BF16),
            pltpu.VMEM((WT, 2, vocab // WT // 2, wide), BF16),
            pltpu.VMEM((WT, 2, vocab // WT // 2, wide), BF16),
            pltpu.VMEM((1, vocab), F32),
            pltpu.VMEM((WT, 1, vocab), F32),
            pltpu.VMEM((WT, 2, vocab // WT // 2, wide), BF16),
            pltpu.VMEM((nseq, 1, BLK), jnp.int32),
            pltpu.VMEM((WT, 1, BLK), jnp.int32),
            pltpu.VMEM((BLK // GSZ * BLK, 2 * BLK), BF16),
            pltpu.VMEM((HALO + 3 * BLK, wide), F32),
            pltpu.VMEM((nchip, 2, BLK, BLK), BF16),
            pltpu.VMEM((nchip, WT, 2, BLK, BLK), BF16),
            pltpu.VMEM((WT * BLK, feats), F32),
            dma,
            dma,
            dma((2, WT)),
            dma((2, WT)),
            dma((WT,)),
            dma((WT,)),
            dma((2, WT)),
            dma((2, WT)),
            dma((nseq,)),
            dma((nseq,)),
            dma((WT,)),
            dma((WT,)),
            dma((nchip, 4)),
            dma((nchip, 4)),
            dma((nchip * 4,)),
            dma((nchip * 4,)),
            dma((nchip * 6,)),
            dma((nchip * 6,)),
        ],
        compiler_params=pltpu.CompilerParams(
            collective_id=0, has_side_effects=True, vmem_limit_bytes=50 * 2**20
        ),
        name="hyena_block",
    )(
        *(
            pltpu.with_memory_space_constraint(x, pltpu.HBM)
            for x in (
                tokens,
                embed_table,
                norm_gain,
                jnp.transpose(w_in, (1, 0, 2)),
                short_taps,
                filters,
                w_out,
            )
        )
    )


def solution(mesh):
    placed = (
        P("wt", "seq"),
        P(None, "wt"),
        P("wt"),
        P("wt", None, "seq"),
        P(None, None, "seq"),
        P("seq", None),
        P("wt", None),
    )
    return jax.shard_map(
        functools.partial(local, mesh.shape["seq"]),
        mesh=mesh,
        in_specs=placed,
        out_specs=P(None, "seq", "wt"),
        check_vma=False,
    )
```
